128 devices in a mesh: seq: 16 (over z, x), ctx: 8 (over y, core).
Axes of the slice: x: 4, y: 4, z: 4, core: 2. Of those that a mesh axis runs over, the one named last changes fastest.
Arguments:
- queries: bfloat16 [8192, 4096], P(('seq', 'ctx')), may hold values from -90 to 90
- stretch_kv: bfloat16 [2, 8192, 1024], P(None, ('seq', 'ctx')), may hold values from -4.1 to 4.1
- cache_kv: bfloat16 [1024, 2, 8, 128, 128], P('ctx', None, None, 'seq'), may hold values from -4 to 4
- vertical: int32 [32, 8], replicated, may hold values from 0 to 1023, as said below
- slash: int32 [32, 24], replicated, may hold values from 0 to 1023
- owner_map: int32 [1024], replicated, may hold values from 0 to 1023, as said below
Outputs:
- attended: bfloat16 [8192, 4096], P(('seq', 'ctx'))
The draws below stay inside these ranges and needn't reach their ends.
Inputs may be any that keep to these rules, and one draw needn't show every extreme that they name: For every head the 8 vertical blocks and the blocks 1024 - 1 - s of its slash entries s are 32 distinct blocks; for every head exactly 12 of them have storage rows in one range g * 128 to (g + 1) * 128 - 1, and at most 3 in each other such range, with exactly 3 in some. `owner_map`: each storage row appears once.
All inputs are finite; a program needn't handle non-finite values.
Results may differ from the reference program's by a relative error of at most 0.0075.
Values may be sent and summed in bfloat16 or wider, within the bound.
A program may use at most 128 MiB of HBM per device.

```python
import math
import jax
import jax.numpy as jnp
from jax import lax

H = 32
KVH = 8
HD = 128
BLK = 128
NV = 8
CAP = 12
BLK_CTX = 128
NSEL = 32
STRETCH = 8192
NBLK = 1024
N_CTX = 8


def attention_inputs(key):
    base = jax.random.fold_in(key, 11)
    key_query, key_keys, key_values = jax.random.split(base, 3)
    query_rows = jax.random.truncated_normal(key_query, -4.0, 4.0, (STRETCH, H, HD), jnp.float32)
    key_rows = jax.random.truncated_normal(key_keys, -4.0, 4.0, (STRETCH, KVH, HD), jnp.float32)
    value_rows = jax.random.truncated_normal(key_values, -4.0, 4.0, (STRETCH, KVH, HD), jnp.float32)
    return (query_rows.reshape(STRETCH, H * HD), jnp.stack([key_rows.reshape(STRETCH, KVH * HD), value_rows.reshape(STRETCH, KVH * HD)]))


def block_lists(key):
    base = jax.random.fold_in(key, 23)
    key_perm, key_heavy, key_rank, key_pick = jax.random.split(base, 4)
    owner_map = jax.random.permutation(key_perm, NBLK).astype(jnp.int32)
    logical_of = jnp.argsort(owner_map).astype(jnp.int32)
    heavy = jax.random.randint(key_heavy, (H, 1), 0, N_CTX)
    others = NSEL - CAP
    spread = others // (N_CTX - 1)
    extra = others - spread * (N_CTX - 1)
    offset = (jnp.arange(N_CTX, dtype=jnp.int32)[None, :] - heavy - 1) % N_CTX
    counts = jnp.where(offset == N_CTX - 1, CAP, spread + (offset < extra).astype(jnp.int32))
    raw_rank = jax.random.randint(key_rank, (H, N_CTX, BLK_CTX), 0, 1 << 20)
    local_order = jnp.argsort(raw_rank * BLK_CTX + jnp.arange(BLK_CTX, dtype=jnp.int32), axis=-1).astype(jnp.int32)
    storage = jnp.arange(N_CTX, dtype=jnp.int32)[None, :, None] * BLK_CTX + local_order
    taken = jnp.arange(BLK_CTX, dtype=jnp.int32)[None, None, :] < counts[:, :, None]
    raw_pick = jax.random.randint(key_pick, (H, N_CTX, BLK_CTX), 0, 1 << 14)
    sort_key = jnp.where(taken, raw_pick, 1 << 14) * NBLK + jnp.arange(NBLK, dtype=jnp.int32).reshape(N_CTX, BLK_CTX)
    first = jnp.argsort(sort_key.reshape(H, NBLK), axis=-1)[:, :NSEL]
    chosen_rows = jnp.take_along_axis(storage.reshape(H, NBLK), first, axis=-1)
    logical = logical_of[chosen_rows]
    return (owner_map, logical[:, :NV].astype(jnp.int32), (NBLK - 1 - logical[:, NV:]).astype(jnp.int32))


def draw_queries(key, part):
    return attention_inputs(key)[0].astype(jnp.bfloat16)


def draw_stretch_kv(key, part):
    return attention_inputs(key)[1].astype(jnp.bfloat16)


def draw_vertical(key, part):
    return block_lists(key)[1]


def draw_slash(key, part):
    return block_lists(key)[2]


def draw_owner_map(key, part):
    return block_lists(key)[0]


def steps_of(rng, extent, cuts, low, high):
    def one(dim, shards_of):
        draws = jax.random.uniform(jax.random.fold_in(jax.random.fold_in(rng, 6), dim), (shards_of,), jnp.float32, low / len(cuts), high / len(cuts))
        return jnp.repeat(jnp.exp(draws), extent[dim] // shards_of).reshape((-1,) + (1,) * (len(extent) - dim - 1))

    gain = one(*cuts[0])
    for cut in cuts[1:]:
        gain = gain * one(*cut)
    return gain


def noise(rng, dims, deviation, limit, pieces=(), held_as=jnp.bfloat16):
    array = deviation * jax.random.normal(rng, dims, jnp.float32)
    if pieces:
        array = array * steps_of(rng, dims, pieces, -0.22, 0.18)
    return jnp.clip(array, -limit, limit).astype(held_as)


def setup_inputs(seed: int = 0) -> dict:
    key_list = jax.random.split(jax.random.key(seed), 7)
    return {
        "queries": draw_queries(jax.random.fold_in(key_list[6], 71), 0),
        "stretch_kv": draw_stretch_kv(jax.random.fold_in(key_list[6], 71), 0),
        "cache_kv": noise(key_list[2], (NBLK, 2, KVH, BLK, HD), 1.0, 4.0, ((0, 8), (3, 16))),
        "vertical": draw_vertical(jax.random.fold_in(key_list[6], 71), 0),
        "slash": draw_slash(jax.random.fold_in(key_list[6], 71), 0),
        "owner_map": draw_owner_map(jax.random.fold_in(key_list[6], 71), 0),
    }


masked_value = -1e30


def reference(queries, stretch_kv, cache_kv, vertical, slash, owner_map):
    selected = jnp.concatenate([vertical, NBLK - 1 - slash], axis=1).astype(jnp.int32)
    storage = owner_map[selected]
    group_size = H // KVH
    query_heads = queries.reshape(STRETCH, H, HD)
    stretch_keys = stretch_kv[0].reshape(STRETCH, KVH, HD)
    stretch_values = stretch_kv[1].reshape(STRETCH, KVH, HD)
    block_rows = math.gcd(STRETCH, 512)
    score_scale = HD ** -0.5
    positions = jnp.arange(STRETCH, dtype=jnp.int32)
    cache_open = jnp.ones((block_rows, NSEL * BLK), dtype=bool)

    def one_head(head):
        kv_head = head // group_size
        cached_keys = cache_kv[storage[head], 0, kv_head].reshape(NSEL * BLK, HD)
        cached_values = cache_kv[storage[head], 1, kv_head].reshape(NSEL * BLK, HD)
        all_keys = jnp.concatenate([cached_keys, lax.dynamic_index_in_dim(stretch_keys, kv_head, 1, keepdims=False)], axis=0)
        all_values = jnp.concatenate([cached_values, lax.dynamic_index_in_dim(stretch_values, kv_head, 1, keepdims=False)], axis=0)
        head_queries = lax.dynamic_index_in_dim(query_heads, head, 1, keepdims=False)

        def one_block(index):
            start = index * block_rows
            block_queries = lax.dynamic_slice_in_dim(head_queries, start, block_rows, 0)
            scores = jnp.dot(block_queries, all_keys.T, preferred_element_type=jnp.float32) * score_scale
            query_position = start + jnp.arange(block_rows, dtype=jnp.int32)
            visible = jnp.concatenate([cache_open, positions[None, :] <= query_position[:, None]], axis=1)
            masked = jnp.where(visible, scores, masked_value)
            peak = jnp.max(masked, axis=1, keepdims=True)
            weights = jnp.where(visible, jnp.exp(masked - peak), 0.0)
            total = jnp.sum(weights, axis=1, keepdims=True)
            mixed = jnp.dot(weights.astype(jnp.bfloat16), all_values, preferred_element_type=jnp.float32)
            return (mixed / total).astype(jnp.bfloat16)

        blocks = lax.map(one_block, jnp.arange(STRETCH // block_rows, dtype=jnp.int32))
        return blocks.reshape(STRETCH, HD)

    heads = lax.map(one_head, jnp.arange(H, dtype=jnp.int32))
    return jnp.transpose(heads, (1, 0, 2)).reshape(STRETCH, H * HD)
```

```python
import jax
import jax.numpy as jnp
from jax import lax
from jax.experimental import pallas as pl
from jax.experimental.pallas import tpu as pltpu
from jax.sharding import PartitionSpec as P

H = 32
KVH = 8
HD = 128
BLK = 128
NSEL = 32
CAP = 12
GROUP = H // KVH
TOK = 64
STRETCH = 8192
LOG2E = 1.4426950408889634
EXP_SCALE = HD**-0.5 * LOG2E
masked_value = -1e30
Q_TILE = 256
K_TILE = 1024
CACHED = NSEL * BLK


def flash_kernel(q_ref, kv_ref, ckv_ref, out_ref):
    tile = pl.program_id(0)
    quarter = lax.rem(lax.axis_index("seq"), 4)
    q = q_ref[...]
    ones = jnp.ones((K_TILE, HD), jnp.bfloat16)

    def step(carry, keys, values, masked):
        peak, acc = carry
        scores = lax.dot_general(q, keys, (((1,), (1,)), ((), ())), preferred_element_type=jnp.float32)
        if masked:
            row = lax.broadcasted_iota(jnp.int32, scores.shape, 0)
            col = lax.broadcasted_iota(jnp.int32, scores.shape, 1)
            limit = row // 128 * 512 + quarter * 128 + row % 128
            scores = jnp.where(col <= limit, scores, masked_value)
        new_peak = jnp.maximum(peak, jnp.max(scores, axis=1, keepdims=True))
        weights = jnp.exp2((scores - new_peak) * EXP_SCALE)
        fading = jnp.exp2((peak - new_peak) * EXP_SCALE)
        mixed = jnp.dot(
            weights.astype(jnp.bfloat16),
            jnp.concatenate([values, ones], axis=1),
            preferred_element_type=jnp.float32,
        )
        return new_peak, acc * fading + mixed

    carry = (
        jnp.full((Q_TILE, 1), masked_value, jnp.float32),
        jnp.zeros((Q_TILE, 2 * HD), jnp.float32),
    )
    for block in range(CACHED // K_TILE):
        rows = pl.ds(block * K_TILE, K_TILE)
        carry = step(carry, ckv_ref[0, rows, :], ckv_ref[1, rows, :], False)

    def full(block, carry):
        rows = pl.ds(pl.multiple_of(block * K_TILE, K_TILE), K_TILE)
        return step(carry, kv_ref[0, rows, :], kv_ref[1, rows, :], False)

    carry = lax.fori_loop(0, tile, full, carry)
    rows = pl.ds(pl.multiple_of(tile * K_TILE, K_TILE), K_TILE)
    peak, acc = step(carry, kv_ref[0, rows, :], kv_ref[1, rows, :], True)
    out_ref[...] = (acc[:, :HD] / acc[:, HD:]).astype(jnp.bfloat16)


def flash(q, kv, ckv):
    return pl.pallas_call(
        flash_kernel,
        grid=(q.shape[0] // Q_TILE,),
        in_specs=[
            pl.BlockSpec((Q_TILE, HD), lambda i: (i, 0)),
            pl.BlockSpec(kv.shape, lambda i: (0, 0, 0), pipeline_mode=pl.Buffered(1)),
            pl.BlockSpec(ckv.shape, lambda i: (0, 0, 0), pipeline_mode=pl.Buffered(1)),
        ],
        out_specs=pl.BlockSpec((Q_TILE, HD), lambda i: (i, 0)),
        out_shape=jax.ShapeDtypeStruct(q.shape, jnp.bfloat16),
        compiler_params=pltpu.CompilerParams(vmem_limit_bytes=48 << 20),
    )(q, kv, ckv)


def block_places(vertical, slash, owner_map, ctx_index):
    nblk = owner_map.shape[0]
    selected = jnp.concatenate([vertical, nblk - 1 - slash], axis=1)
    hit = selected[:, :, None] == jnp.arange(nblk, dtype=jnp.int32)
    storage = jnp.sum(jnp.where(hit, owner_map, 0), axis=2)
    per_ctx = nblk // 8
    owner = storage // per_ctx
    local_row = storage % per_ctx
    order = jnp.arange(NSEL, dtype=jnp.int32)
    earlier = (owner[:, :, None] == owner[:, None, :]) & (order[None, None, :] < order[None, :, None])
    rank = jnp.sum(earlier.astype(jnp.int32), axis=2)
    slot_hit = (owner[:, :, None] == ctx_index) & (rank[:, :, None] == jnp.arange(CAP, dtype=jnp.int32))
    send_rows = jnp.sum(jnp.where(slot_hit, local_row[:, :, None], 0), axis=1)
    in_group = jnp.arange(H, dtype=jnp.int32)[:, None] % GROUP
    places = (owner * GROUP + in_group) * CAP + rank
    return send_rows, places


def on_device(queries, stretch_kv, cache_kv, vertical, slash, owner_map):
    ctx_index = lax.axis_index("ctx")
    send_rows, places = block_places(vertical, slash, owner_map, ctx_index)
    own_places = lax.dynamic_slice_in_dim(places, ctx_index * GROUP, GROUP, 0)
    group_of = jnp.arange(H, dtype=jnp.int32)[:, None] // GROUP
    columns = [[z * 4 + x for z in range(4)] for x in range(4)]
    rows = [[z * 4 + x for x in range(4)] for z in range(4)]

    own_kv = lax.all_to_all(stretch_kv.reshape(2, TOK, KVH, HD), "ctx", split_axis=2, concat_axis=1, tiled=True)
    own_kv = own_kv.reshape(2, 8 * TOK, HD)
    kv = lax.all_gather(own_kv, "seq", axis=1, tiled=True)
    packed = cache_kv[send_rows, :, group_of]
    packed = packed.reshape(KVH, GROUP * CAP, 2, 8, HD)
    received = lax.all_to_all(packed, "ctx", split_axis=0, concat_axis=0, tiled=True)
    compact = received.reshape(KVH * GROUP * CAP, 2, 8, HD)[own_places]
    compact = jnp.transpose(compact, (0, 2, 1, 3, 4))
    by_head = lax.all_to_all(compact, "seq", split_axis=0, concat_axis=0, tiled=True, axis_index_groups=columns)
    by_head = by_head.reshape(4, 2, NSEL * 8, HD)
    by_head = jnp.transpose(by_head, (1, 0, 2, 3)).reshape(2, 4 * NSEL * 8, HD)
    ckv = lax.all_gather(by_head, "seq", axis=1, tiled=True, axis_index_groups=rows)

    q = lax.all_to_all(queries.reshape(TOK, KVH, GROUP * HD), "ctx", split_axis=1, concat_axis=0, tiled=True)
    q = q.reshape(4, 2 * TOK, GROUP, HD)
    q = jnp.transpose(q, (2, 0, 1, 3)).reshape(16, 2 * TOK, HD)
    q = lax.all_to_all(q, "seq", split_axis=0, concat_axis=0, tiled=True)
    out = flash(q.reshape(16 * 2 * TOK, HD), kv, ckv)
    out = lax.all_to_all(out.reshape(16, 2 * TOK, HD), "seq", split_axis=0, concat_axis=0, tiled=True)
    out = jnp.transpose(out.reshape(GROUP, 8 * TOK, HD), (1, 0, 2)).reshape(8 * TOK, 1, GROUP * HD)
    out = lax.all_to_all(out, "ctx", split_axis=0, concat_axis=1, tiled=True)
    return out.reshape(TOK, H * HD)


def solution(mesh):
    placed = (
        P(("seq", "ctx"), None),
        P(None, ("seq", "ctx"), None),
        P("ctx", None, None, "seq", None),
        P(),
        P(),
        P(),
    )
    return jax.shard_map(
        on_device, mesh=mesh, in_specs=placed, out_specs=P(("seq", "ctx"), None), check_vma=False
    )
```

```python
import jax
import jax.numpy as jnp
from jax import lax
from jax.experimental import pallas as pl
from jax.experimental.pallas import tpu as pltpu
from jax.sharding import PartitionSpec as P

H = 32
KVH = 8
HD = 128
BLK = 128
NSEL = 32
CAP = 12
GROUP = H // KVH
TOK = 64
STRETCH = 8192
LOG2E = 1.4426950408889634
EXP_SCALE = HD**-0.5 * LOG2E
masked_value = -1e30
Q_TILE = 256
K_TILE = 1024
CACHED = NSEL * BLK


MESH = pl.DeviceIdType.MESH


def remote(src, dst, send_sem, recv_sem, seq, ctx):
    return pltpu.make_async_remote_copy(
        src_ref=src, dst_ref=dst, send_sem=send_sem, recv_sem=recv_sem, device_id=(seq, ctx), device_id_type=MESH
    )


def comm_kernel(
    rows_ref, places_ref, queries, stretch, cache, q_out, kv_out, ckv_out,
    cache_v, packed, arrived, compact, q_mid,
    kv_send, kv_recv, q_send, q_recv, c_send, c_recv, qb_send, qb_recv,
    p1_send, p1_recv, p2_send, p2_recv, cz_send, cz_recv, cx_send, cx_recv, local_sem,
):
    seq, ctx = lax.axis_index("seq"), lax.axis_index("ctx")
    z, x = seq // 4, seq % 4

    def along(axis, delta):
        if axis == "x":
            return z * 4 + (x + delta + 4) % 4
        return (z + delta + 4) % 4 * 4 + x

    barrier = pltpu.get_barrier_semaphore()
    for d in range(1, 8):
        pl.semaphore_signal(barrier, inc=1, device_id=(seq, (ctx + d) % 8), device_id_type=MESH)
    for d in range(1, 16):
        pl.semaphore_signal(barrier, inc=1, device_id=((seq + d) % 16, ctx), device_id_type=MESH)
    load_cache = pltpu.make_async_copy(cache, cache_v, local_sem.at[0])
    load_cache.start()
    pl.semaphore_wait(barrier, 22)

    def lane(index, size):
        return pl.ds(pl.multiple_of(index * size, size), size)

    def kv_a(d, from_ctx, to_ctx):
        return (
            stretch.at[:, :, lane(to_ctx, HD)],
            kv_out.at[:, pl.ds(pl.multiple_of(seq * 512 + from_ctx * TOK, TOK), TOK), :],
        )

    def q_a(d, from_ctx, to_ctx):
        return queries.at[:, lane(to_ctx, GROUP * HD)], q_mid.at[lane(from_ctx, TOK), :]

    sends = []
    for d in range(1, 8):
        peer = (ctx + d) % 8
        sends.append(remote(*kv_a(d, ctx, peer), kv_send.at[d], kv_recv.at[d], seq, peer))
        sends[-1].start()
    own_kv = pltpu.make_async_copy(*kv_a(0, ctx, ctx), local_sem.at[1])
    own_kv.start()
    for d in range(1, 8):
        peer = (ctx + d) % 8
        sends.append(remote(*q_a(d, ctx, peer), q_send.at[d], q_recv.at[d], seq, peer))
        sends[-1].start()
    own_q = pltpu.make_async_copy(*q_a(0, ctx, ctx), local_sem.at[2])
    own_q.start()

    load_cache.wait()
    for d in range(8):
        peer = (ctx + d) % 8

        def pack(member, carry, peer=peer):
            base = (peer * GROUP + member) * CAP
            for slot in range(CAP):
                packed[base + slot] = cache_v[rows_ref[base + slot], :, peer]
            return carry

        lax.fori_loop(0, GROUP, pack, 0)
        if d:
            sends.append(
                remote(
                    packed.at[pl.ds(peer * GROUP * CAP, GROUP * CAP)],
                    arrived.at[pl.ds(ctx * GROUP * CAP, GROUP * CAP)],
                    c_send.at[d], c_recv.at[d], seq, peer,
                )
            )
            sends[-1].start()
        else:
            own_c = pltpu.make_async_copy(
                packed.at[pl.ds(peer * GROUP * CAP, GROUP * CAP)],
                arrived.at[pl.ds(ctx * GROUP * CAP, GROUP * CAP)],
                local_sem.at[3],
            )
            own_c.start()

    own_kv.wait()
    for d in range(1, 8):
        origin = (ctx - d + 8) % 8
        remote(*kv_a(d, origin, ctx), kv_send.at[d], kv_recv.at[d], seq, origin).wait_recv()

    axes = (("x", "z"), ("z", "x"))
    OFFSETS = (0, -1, 1, 2)

    def kv_block(i, s, half=None):
        if half is None:
            return kv_out.at[i, pl.ds(pl.multiple_of(s * 512, 512), 512), :]
        return kv_out.at[i, pl.ds(pl.multiple_of(s * 512 + half * 256, 256), 256), :]

    def at(i, first, second):
        dx, dz = (first, second) if i == 0 else (second, first)
        return (z + dz + 4) % 4 * 4 + (x + dx + 4) % 4

    def first_hop(i, j):
        step = (1, -1, 1, -1)[j]
        block = (0, 0, -1, 1)[j]
        half = (None, None, 0, 1)[j]
        return step, block, half

    def p1(i, j):
        step, block, half = first_hop(i, j)
        ref = kv_block(i, at(i, block, 0), half)
        return remote(ref, ref, p1_send.at[i, j], p1_recv.at[i, j], along(axes[i][0], step), ctx)

    def p1_in(i, j):
        step, block, half = first_hop(i, j)
        ref = kv_block(i, at(i, block - step, 0), half)
        return remote(ref, ref, p1_send.at[i, j], p1_recv.at[i, j], along(axes[i][0], step), ctx)

    def p2(i, p, j):
        step, block, half = first_hop(i, j)
        ref = kv_block(i, at(i, OFFSETS[p], block), half)
        return remote(ref, ref, p2_send.at[i, p, j], p2_recv.at[i, p, j], along(axes[i][1], step), ctx)

    def p2_in(i, p, j):
        step, block, half = first_hop(i, j)
        ref = kv_block(i, at(i, OFFSETS[p], block - step), half)
        return remote(ref, ref, p2_send.at[i, p, j], p2_recv.at[i, p, j], along(axes[i][1], step), ctx)

    def go(copy):
        copy.start()
        sends.append(copy)

    for i in range(2):
        go(p1(i, 0))
        go(p1(i, 1))
    for i in range(2):
        go(p2(i, 0, 0))
        go(p2(i, 0, 1))

    own_q.wait()
    for d in range(1, 8):
        origin = (ctx - d + 8) % 8
        remote(*q_a(d, origin, ctx), q_send.at[d], q_recv.at[d], seq, origin).wait_recv()

    def q_part(target):
        return q_mid.at[lane(target % 4, 128), lane(target // 4, HD)]

    for d in range(1, 16):
        target = (seq + d) % 16
        go(remote(q_part(target), q_out.at[seq], qb_send.at[d], qb_recv.at[d], target, ctx))
    own_qb = pltpu.make_async_copy(q_part(seq), q_out.at[seq], local_sem.at[4])
    own_qb.start()

    for j in range(2):
        for i in range(2):
            p1_in(i, j).wait_recv()
            go(p1(i, 2 + j))
            go(p2(i, 1 + j, 0))
            go(p2(i, 1 + j, 1))
    for j in range(2):
        for i in range(2):
            p2_in(i, 0, j).wait_recv()
            go(p2(i, 0, 2 + j))
    for i in range(2):
        p1_in(i, 2).wait_recv()
        p1_in(i, 3).wait_recv()
        go(p2(i, 3, 0))
        go(p2(i, 3, 1))
    for p in (1, 2):
        for j in range(2):
            for i in range(2):
                p2_in(i, p, j).wait_recv()
                go(p2(i, p, 2 + j))

    own_c.wait()
    for d in range(1, 8):
        origin = (ctx - d + 8) % 8
        remote(
            packed.at[pl.ds(ctx * GROUP * CAP, GROUP * CAP)],
            arrived.at[pl.ds(origin * GROUP * CAP, GROUP * CAP)],
            c_send.at[d], c_recv.at[d], seq, origin,
        ).wait_recv()

    def ckv_part(dx, dz, half=None):
        index = (x + dx + 4) % 4 * 4 + (z + dz + 4) % 4
        if half is None:
            return ckv_out.at[:, index]
        return ckv_out.at[:, index, pl.ds(half * 16, 16)]

    def squeeze(member):
        def body(step, carry):
            for k in range(8):
                n = step * 8 + k
                block = arrived[places_ref[member * NSEL + n]]
                compact[member, 0, n] = block[0]
                compact[member, 1, n] = block[1]
            return carry

        lax.fori_loop(0, NSEL // 8, body, 0)

    for dz in (2, 1, 3, 0):
        member = (z + dz) % 4
        squeeze(member)
        if dz:
            go(remote(compact.at[member], ckv_part(0, 0), cz_send.at[dz], cz_recv.at[dz], member * 4 + x, ctx))
        else:
            own_z = pltpu.make_async_copy(compact.at[member], ckv_part(0, 0), local_sem.at[5])
            own_z.start()

    for j in range(2):
        for i in range(2):
            p2_in(i, 3, j).wait_recv()
            go(p2(i, 3, 2 + j))

    def cx(dz, j):
        step, block, half = first_hop(0, j)
        ref = ckv_part(block, dz, half)
        return remote(ref, ref, cx_send.at[dz, j], cx_recv.at[dz, j], along("x", step), ctx)

    def cx_in(dz, j):
        step, block, half = first_hop(0, j)
        ref = ckv_part(block - step, dz, half)
        return remote(ref, ref, cx_send.at[dz, j], cx_recv.at[dz, j], along("x", step), ctx)

    order = (0, 3, 1, 2)
    for dz in order:
        if dz:
            ref = ckv_part(0, -dz)
            remote(compact.at[0], ref, cz_send.at[dz], cz_recv.at[dz], along("z", -dz), ctx).wait_recv()
        else:
            own_z.wait()
        go(cx((4 - dz) % 4, 0))
        go(cx((4 - dz) % 4, 1))
    for dz in order:
        for j in range(2):
            cx_in((4 - dz) % 4, j).wait_recv()
            go(cx((4 - dz) % 4, 2 + j))

    for p in range(4):
        for i in range(2):
            p2_in(i, p, 2).wait_recv()
            p2_in(i, p, 3).wait_recv()
    own_qb.wait()
    for d in range(1, 16):
        origin = (seq - d + 16) % 16
        remote(q_part(seq), q_out.at[origin], qb_send.at[d], qb_recv.at[d], origin, ctx).wait_recv()
    for dz in order:
        for j in (2, 3):
            cx_in((4 - dz) % 4, j).wait_recv()
    for copy in sends:
        copy.wait_send()


def exchange(send_rows, places, queries, stretch, cache):
    any_space = pl.BlockSpec(memory_space=pl.ANY)
    smem = pl.BlockSpec(memory_space=pltpu.SMEM)
    dma = pltpu.SemaphoreType.DMA
    bf16 = jnp.bfloat16
    return pl.pallas_call(
        comm_kernel,
        in_specs=[smem, smem, any_space, any_space, any_space],
        out_specs=[any_space] * 3,
        out_shape=[
            jax.ShapeDtypeStruct((16, 128, HD), bf16),
            jax.ShapeDtypeStruct((2, STRETCH, HD), bf16),
            jax.ShapeDtypeStruct((2, 16, NSEL, 8, HD), bf16),
        ],
        scratch_shapes=[
            pltpu.VMEM(cache.shape, bf16),
            pltpu.VMEM((H * CAP, 2, 8, HD), bf16),
            pltpu.VMEM((H * CAP, 2, 8, HD), bf16),
            pltpu.VMEM((GROUP, 2, NSEL, 8, HD), bf16),
            pltpu.VMEM((8 * TOK, GROUP * HD), bf16),
            dma((8,)), dma((8,)), dma((8,)), dma((8,)), dma((8,)), dma((8,)), dma((16,)), dma((16,)),
            dma((2, 4)), dma((2, 4)), dma((2, 4, 4)), dma((2, 4, 4)), dma((4,)), dma((4,)), dma((4, 4)), dma((4, 4)),
            dma((6,)),
        ],
        compiler_params=pltpu.CompilerParams(collective_id=0, has_side_effects=True, vmem_limit_bytes=40 << 20),
    )(send_rows, places, queries, stretch, cache)


def attend(q, carry, keys, values, limit):
    peak, acc = carry
    scores = lax.dot_general(q, keys, (((1,), (1,)), ((), ())), preferred_element_type=jnp.float32)
    if limit is not None:
        scores = jnp.where(lax.broadcasted_iota(jnp.int32, scores.shape, 1) <= limit, scores, masked_value)
    new_peak = jnp.maximum(peak, jnp.max(scores, axis=1, keepdims=True))
    weights = jnp.exp2((scores - new_peak) * EXP_SCALE)
    fading = jnp.exp2((peak - new_peak) * EXP_SCALE)
    mixed = jnp.dot(
        weights.astype(jnp.bfloat16),
        jnp.concatenate([values, jnp.ones((keys.shape[0], HD), jnp.bfloat16)], axis=1),
        preferred_element_type=jnp.float32,
    )
    return new_peak, acc * fading + mixed


def flash_kernel(q_ref, kv_ref, ckv_ref, out_ref, own, send_sem, recv_sem, local_sem):
    seq, ctx = lax.axis_index("seq"), lax.axis_index("ctx")
    member, quarter = seq // 4, seq % 4
    head = ctx * GROUP + member

    barrier = pltpu.get_barrier_semaphore()
    for other in range(GROUP):
        for group in range(KVH):
            origin = other * 4 + ctx // 2

            @pl.when((origin != seq) | (group != ctx))
            def _(origin=origin, group=group):
                pl.semaphore_signal(barrier, inc=1, device_id=(origin, group), device_id_type=MESH)

    mine = quarter == ctx // 2

    def column(index):
        return pl.ds(pl.multiple_of(index * HD, HD), HD)

    def give(piece, half):
        source = own.at[piece, pl.ds(half * TOK, TOK), :]
        return remote(
            source, out_ref.at[:, column(head)], send_sem.at[piece, half], recv_sem.at[member, ctx],
            piece, quarter * 2 + half,
        )

    def is_self(piece, half):
        return (piece == seq) & (quarter * 2 + half == ctx)

    row = lax.broadcasted_iota(jnp.int32, (Q_TILE, 1), 0)
    limit = row // 128 * 512 + quarter * 128 + row % 128

    for tile in reversed(range(16 * 128 // Q_TILE)):
        q = q_ref[pl.ds(tile * Q_TILE, Q_TILE), :]
        carry = (
            jnp.full((Q_TILE, 1), masked_value, jnp.float32),
            jnp.zeros((Q_TILE, 2 * HD), jnp.float32),
        )

        def cached(block, carry, q=q):
            rows = pl.ds(pl.multiple_of(block * K_TILE, K_TILE), K_TILE)
            return attend(q, carry, ckv_ref[0, rows, :], ckv_ref[1, rows, :], None)

        def full(block, carry, q=q):
            rows = pl.ds(pl.multiple_of(block * K_TILE, K_TILE), K_TILE)
            return attend(q, carry, kv_ref[0, rows, :], kv_ref[1, rows, :], None)

        carry = lax.fori_loop(0, CACHED // K_TILE, cached, carry)
        carry = lax.fori_loop(0, tile, full, carry)
        rows = pl.ds(tile * K_TILE, K_TILE)
        peak, acc = attend(q, carry, kv_ref[0, rows, :], kv_ref[1, rows, :], limit)
        own[pl.ds(tile * 2, 2)] = (acc[:, :HD] / acc[:, HD:]).astype(jnp.bfloat16).reshape(2, 128, HD)
        if tile == 16 * 128 // Q_TILE - 1:
            pl.semaphore_wait(barrier, 32 - mine.astype(jnp.int32))
        for piece in (2 * tile, 2 * tile + 1):
            for half in range(2):
                @pl.when(jnp.logical_not(is_self(piece, half)))
                def _(piece=piece, half=half):
                    give(piece, half).start()

                @pl.when(is_self(piece, half))
                def _(piece=piece, half=half):
                    pltpu.make_async_copy(
                        own.at[piece, pl.ds(half * TOK, TOK), :], out_ref.at[:, column(head)], local_sem
                    ).start()

    for piece in range(16):
        for half in range(2):
            @pl.when(jnp.logical_not(is_self(piece, half)))
            def _(piece=piece, half=half):
                give(piece, half).wait_send()

            @pl.when(is_self(piece, half))
            def _(piece=piece, half=half):
                pltpu.make_async_copy(
                    own.at[piece, pl.ds(half * TOK, TOK), :], out_ref.at[:, column(head)], local_sem
                ).wait()
    for other in range(GROUP):
        for group in range(KVH):
            origin = other * 4 + ctx // 2

            @pl.when((origin != seq) | (group != ctx))
            def _(other=other, group=group, origin=origin):
                remote(
                    own.at[0, pl.ds(0, TOK), :], out_ref.at[:, pl.ds((group * GROUP + other) * HD, HD)],
                    send_sem.at[0, 0], recv_sem.at[other, group], origin, group,
                ).wait_recv()


def flash(q, kv, ckv):
    vmem = pl.BlockSpec(memory_space=pltpu.VMEM)
    dma = pltpu.SemaphoreType.DMA
    return pl.pallas_call(
        flash_kernel,
        in_specs=[vmem] * 3,
        out_specs=pl.BlockSpec(memory_space=pl.ANY),
        out_shape=jax.ShapeDtypeStruct((TOK, H * HD), jnp.bfloat16),
        scratch_shapes=[
            pltpu.VMEM((16, 128, HD), jnp.bfloat16),
            dma((16, 2)), dma((GROUP, KVH)), dma,
        ],
        compiler_params=pltpu.CompilerParams(collective_id=1, has_side_effects=True, vmem_limit_bytes=48 << 20),
    )(q, kv, ckv)


def block_places(vertical, slash, owner_map, ctx_index):
    nblk = owner_map.shape[0]
    selected = jnp.concatenate([vertical, nblk - 1 - slash], axis=1)
    hit = selected[:, :, None] == jnp.arange(nblk, dtype=jnp.int32)
    storage = jnp.sum(jnp.where(hit, owner_map, 0), axis=2)
    per_ctx = nblk // 8
    owner = storage // per_ctx
    local_row = storage % per_ctx
    order = jnp.arange(NSEL, dtype=jnp.int32)
    earlier = (owner[:, :, None] == owner[:, None, :]) & (order[None, None, :] < order[None, :, None])
    rank = jnp.sum(earlier.astype(jnp.int32), axis=2)
    slot_hit = (owner[:, :, None] == ctx_index) & (rank[:, :, None] == jnp.arange(CAP, dtype=jnp.int32))
    send_rows = jnp.sum(jnp.where(slot_hit, local_row[:, :, None], 0), axis=1)
    in_group = jnp.arange(H, dtype=jnp.int32)[:, None] % GROUP
    places = (owner * GROUP + in_group) * CAP + rank
    return send_rows, places


def on_device(queries, stretch_kv, cache_kv, vertical, slash, owner_map):
    ctx_index = lax.axis_index("ctx")
    send_rows, places = block_places(vertical, slash, owner_map, ctx_index)
    own_places = lax.dynamic_slice_in_dim(places, ctx_index * GROUP, GROUP, 0)
    q, kv, ckv = exchange(send_rows.reshape(-1), own_places.reshape(-1), queries, stretch_kv, cache_kv)
    return flash(q.reshape(16 * 128, HD), kv, ckv.reshape(2, CACHED, HD))


def solution(mesh):
    placed = (
        P(("seq", "ctx"), None),
        P(None, ("seq", "ctx"), None),
        P("ctx", None, None, "seq", None),
        P(),
        P(),
        P(),
    )
    return jax.shard_map(
        on_device, mesh=mesh, in_specs=placed, out_specs=P(("seq", "ctx"), None), check_vma=False
    )
```
